256 devices in a mesh: dp: 8 (over x_hi, y), row: 4 (over x_lo, core), col: 8 (over z).
Axes of the slice: x: 4 (x_hi: 2, x_lo: 2; x = x_hi * 2 + x_lo), y: 4, z: 8, core: 2. Of those that a mesh axis runs over, the one named last changes fastest.
Arguments:
- tokens: bfloat16 [32768, 2048], P(('dp', 'row', 'col')), parts along dimension 0, may hold values from -6 to 6
- routes: int32 [32768, 8], P(('dp', 'row', 'col')), parts along dimension 0, may hold values from 0 to 31, all different within a row; in each aligned block of 128 rows (0 to 127, 128 to 255, ...) at most 40 rows name the same one
- gate_values: float32 [32768, 8], P(('dp', 'row', 'col')), parts along dimension 0, may hold values from 0.05 to 1
- w_gate: bfloat16 [32, 2048, 768], P(('row', 'col')), may hold values from -0.125 to 0.125
- w_up: bfloat16 [32, 2048, 768], P(('row', 'col')), may hold values from -0.125 to 0.125
- w_down: bfloat16 [32, 768, 2048], P(('row', 'col')), may hold values from -0.21875 to 0.21875
Outputs:
- combined: bfloat16 [32768, 2048], P(('dp', 'row', 'col')), parts along dimension 0
The draws below stay inside these ranges and needn't reach their ends.
There are 8 independent parts, one for each index of `dp`. The reference program is written for one: setup_inputs(seed, part) draws one part's arguments, and reference() takes and returns one part's arrays. A program takes and returns all parts, laid end to end along the dimension named above; an argument that names none is the same for every part. Nothing has to cross between parts.
Inputs may be any that keep to these rules, and one draw needn't show every extreme that they name: `routes`: each row names 8 different experts; among the rows of one device no expert is named more than 40 times, a bound that some block reaches.
All inputs are finite; a program needn't handle non-finite values.
Results may differ from the reference program's by a relative error of at most 0.0057.
Values may be sent and summed in bfloat16 or wider, within the bound.
No kernel may reach another device: no remote copies, remote signals or barrier semaphores. Data moves between devices by JAX's collectives and lax.ppermute only.
A program may use at most 128 MiB of HBM per device.

```python
import math
import jax
import jax.numpy as jnp
import numpy as np
from jax import lax

D = 2048
FF = 768
TOPK = 8
TOK_DEV = 128
EXPERTS = 32
TOKENS = 4096
CAP = 40
N_ROW = 4
N_COL = 8


def block_scale(own_key, shape, split, low, high):
    def one(position, shards_of):
        heights = jax.random.uniform(jax.random.fold_in(jax.random.fold_in(own_key, 6), position), (shards_of,), jnp.float32, low / len(split), high / len(split))
        return jnp.repeat(jnp.exp(heights), shape[position] // shards_of).reshape((-1,) + (1,) * (len(shape) - position - 1))

    loudness = one(*split[0])
    for cut in split[1:]:
        loudness = loudness * one(*cut)
    return loudness


def routed_block(rng, own, number, rows, count, top, limit, slope):
    sequence = jax.random.permutation(rng, count)
    packed, ordinary = load_shares(count, rows * top, limit, slope, True), load_shares(count, rows * top, limit, slope, False)
    places = jnp.arange(count)

    def named(tallies, rotation):
        used = int((tallies > 0).sum())
        fixed = max(1, used // 4)
        passed = fixed + (places - fixed + rotation * (used - fixed)) % max(1, count - fixed)
        return jnp.zeros((count,), jnp.int32).at[sequence[jnp.where(places < fixed, places, passed)]].set(jnp.asarray(tallies, jnp.int32))

    tallies = jnp.where(number % 4 == 0, named(packed, number // 4), named(ordinary, number - number // 4 - 1))
    mixed = jax.random.permutation(jax.random.fold_in(own, 3), count)
    donor, taker = mixed[0:count // 2 * 2:2], mixed[1:count // 2 * 2:2]
    slack = jnp.minimum(tallies[donor] - 1, limit - tallies[taker]) // 2
    slack = jnp.where((donor == sequence[0]) | (taker == sequence[0]) | (tallies[taker] == 0), 0, jnp.maximum(slack, 0))
    passed = jax.random.randint(jax.random.fold_in(own, 4), (count // 2,), 0, 1 << 20) % (slack + 1)
    tallies = tallies.at[donor].add(-passed).at[taker].add(passed)
    labels = jnp.searchsorted(jnp.cumsum(tallies), jnp.arange(rows * top), side="right").astype(jnp.int32)
    listing = labels.reshape(top, rows).T
    listing = listing[jax.random.permutation(jax.random.fold_in(own, 1), rows)]
    rotation = jax.random.randint(jax.random.fold_in(own, 2), (rows, 1), 0, top)
    return jnp.take_along_axis(listing, (jnp.arange(top)[None, :] + rotation) % top, axis=1)


def load_shares(count, total, reach, lean, full):
    portions = [(1 << 20) // math.isqrt(rank ** lean) + 1 for rank in range(1, count + 1)]
    largest = reach if full else min(reach, max(-(-total // count), total * portions[0] // sum(portions)))
    least = 1 if total - largest >= count - 1 else 0
    given, rest = [largest] + [least] * (count - 1), total - largest - least * (count - 1)
    while rest > 0:
        movable = [i for i in range(1, count) if given[i] < largest] or [i for i in range(1, count) if given[i] < reach]
        mass, budget = sum([portions[i] for i in movable]), rest
        for i in movable:
            addition = min(reach - given[i], max(1, budget * portions[i] // mass), rest)
            given[i] = given[i] + addition
            rest = rest - addition
    return np.array(given)


def gaussian(key, dims, scale, bound, cuts=(), kind=jnp.bfloat16):
    factor_of = block_scale(key, dims, cuts, -0.22, 0.18) if cuts else 1.0
    result = jax.random.normal(key, dims, jnp.float32) * scale * factor_of
    return jnp.minimum(jnp.maximum(result, -bound), bound).astype(kind)


def setup_inputs(seed: int = 0, part: int = 0) -> dict:
    key_of = jax.random.split(jax.random.key(seed), 7)
    part_splits = jax.random.split(jax.random.fold_in(key_of[6], part), 7)
    tokens = gaussian(part_splits[0], (TOKENS, D), 1.0, 6.0, ((0, 32),))
    routes_keys = jax.random.split(jax.random.fold_in(part_splits[1], 1), TOKENS // TOK_DEV)
    routes_turns = jax.random.permutation(jax.random.fold_in(part_splits[1], 3), TOKENS // TOK_DEV)
    routes = jax.vmap(lambda own, number: routed_block(jax.random.fold_in(part_splits[1], 2), own, number, TOK_DEV, EXPERTS, TOPK, CAP, 1))(routes_keys, routes_turns).reshape((TOKENS, TOPK))
    gate_values = jnp.clip(jnp.exp(math.log(1.0) - 2.9957323 * jax.random.uniform(part_splits[2], (TOKENS, TOPK), jnp.float32) ** block_scale(part_splits[2], (TOKENS, TOPK), ((0, 32),), -0.2, 0.2)), 0.05, 1.0)
    w_gate = gaussian(key_of[3], (EXPERTS, D, FF), D ** -0.5, 0.125, ((0, 32),))
    w_up = gaussian(key_of[4], (EXPERTS, D, FF), D ** -0.5, 0.125, ((0, 32),))
    w_down = gaussian(key_of[5], (EXPERTS, FF, D), FF ** -0.5, 0.21875, ((0, 32),))
    return dict(tokens=tokens, routes=routes, gate_values=gate_values, w_gate=w_gate, w_up=w_up, w_down=w_down)


def reference(tokens, routes, gate_values, w_gate, w_up, w_down):
    flat_ids = routes.reshape(-1)
    flat_gates = gate_values.reshape(-1)
    slot_limit = N_ROW * N_COL * CAP
    positions = jnp.arange(slot_limit, dtype=jnp.int32)

    def accumulate(total, inputs):
        expert_id, gate_matrix, up_matrix, down_matrix = inputs
        is_hit = flat_ids == expert_id
        hit_count = jnp.sum(is_hit.astype(jnp.int32))
        chosen = jnp.nonzero(is_hit, size=slot_limit, fill_value=0)[0].astype(jnp.int32)
        is_valid = positions < hit_count
        weights = jnp.where(is_valid, flat_gates[chosen], jnp.float32(0.0))
        owners = chosen // TOPK
        gathered = tokens[owners]
        gate_part = jnp.dot(gathered, gate_matrix, preferred_element_type=jnp.float32)
        up_part = jnp.dot(gathered, up_matrix, preferred_element_type=jnp.float32)
        hidden = (jax.nn.silu(gate_part) * up_part).astype(jnp.bfloat16)
        expert_out = jnp.dot(hidden, down_matrix, preferred_element_type=jnp.float32).astype(jnp.bfloat16)
        total = total.at[owners].add(weights[:, None] * expert_out.astype(jnp.float32))
        return total, None

    start = jnp.zeros((TOKENS, D), jnp.float32)
    expert_list = jnp.arange(EXPERTS, dtype=jnp.int32)
    total, unused = lax.scan(accumulate, start, (expert_list, w_gate, w_up, w_down))
    return total.astype(jnp.bfloat16)
```

```python
import jax
import jax.numpy as jnp
from jax import lax
from jax.sharding import PartitionSpec as P


def expert_rows(gathered, w_gate, w_up, w_down):
    gate_part = jnp.dot(gathered, w_gate[0], preferred_element_type=jnp.float32)
    up_part = jnp.dot(gathered, w_up[0], preferred_element_type=jnp.float32)
    hidden = (jax.nn.silu(gate_part) * up_part).astype(jnp.bfloat16)
    return jnp.dot(hidden, w_down[0], preferred_element_type=jnp.float32).astype(jnp.bfloat16)


def slot_numbers(routes, experts):
    tok_rows = routes.shape[0]
    expert_list = jnp.arange(experts, dtype=jnp.int32)
    onehot = (routes[:, :, None] == expert_list).astype(jnp.float32)
    named = jnp.sum(onehot, axis=1)
    order = jnp.arange(tok_rows, dtype=jnp.int32)
    earlier = (order[None, :] < order[:, None]).astype(jnp.bfloat16)
    before = jnp.dot(earlier, named.astype(jnp.bfloat16), preferred_element_type=jnp.float32)
    return jnp.sum(before[:, None, :] * onehot, axis=2).astype(jnp.int32)


def body(tokens, routes, gate_values, w_gate, w_up, w_down):
    tok_rows, features = tokens.shape
    top_count = routes.shape[1]
    row_count = lax.axis_size("row")
    col_count = lax.axis_size("col")
    experts = row_count * col_count
    capacity = 5 * tok_rows * top_count // (4 * experts)
    slots_all = experts * capacity
    flat_ids = routes.reshape(-1)
    slot_index = slot_numbers(routes, experts).reshape(-1)
    destination = flat_ids * capacity + slot_index
    slot_ids = jnp.arange(slots_all, dtype=jnp.int32)
    dest_grid = destination.reshape(tok_rows, top_count)
    hit_table = jnp.any(dest_grid[None, :, :] == slot_ids[:, None, None], axis=2)
    buffer = jnp.dot(
        hit_table.astype(jnp.bfloat16), tokens, preferred_element_type=jnp.float32
    ).astype(jnp.bfloat16)
    received = lax.all_to_all(
        buffer.reshape(experts, capacity, features),
        ("row", "col"),
        split_axis=0,
        concat_axis=0,
        tiled=True,
    )
    item_count = received.shape[1]
    results = expert_rows(received.reshape(-1, features), w_gate, w_up, w_down)
    results = results.reshape(experts, item_count, features)
    returned = lax.all_to_all(results, ("row", "col"), split_axis=0, concat_axis=0, tiled=True)
    picked = jnp.take(returned.reshape(slots_all, features), destination, axis=0)
    picked = picked.reshape(tok_rows, top_count, features)
    combined = jnp.sum(gate_values[:, :, None] * picked, axis=1)
    return combined.astype(jnp.bfloat16)


def solution(mesh):
    placed = (
        P(("dp", "row", "col"), None),
        P(("dp", "row", "col"), None),
        P(("dp", "row", "col"), None),
        P(("row", "col"), None, None),
        P(("row", "col"), None, None),
        P(("row", "col"), None, None),
    )
    return jax.shard_map(
        body, mesh=mesh, in_specs=placed, out_specs=P(("dp", "row", "col"), None), check_vma=False
    )
```

```python
import jax
import jax.numpy as jnp
from jax import lax
from jax.sharding import PartitionSpec as P

F32 = jnp.float32
BF16 = jnp.bfloat16


def expert_rows(rows, w_gate, w_up, w_down):
    gate_part = jnp.dot(rows, w_gate, preferred_element_type=F32)
    up_part = jnp.dot(rows, w_up, preferred_element_type=F32)
    hidden = (jax.nn.silu(gate_part) * up_part).astype(BF16)
    return jnp.dot(hidden, w_down, preferred_element_type=F32).astype(BF16)


def ring(count, step):
    return [(i, (i + step) % count) for i in range(count)]


def swap(count, mask):
    return [(i, i ^ mask) for i in range(count)]


def body(tokens, routes, gate_values, w_gate, w_up, w_down):
    tok_rows, features = tokens.shape
    top_count = routes.shape[1]
    row_count = lax.axis_size("row")
    col_count = lax.axis_size("col")
    experts = row_count * col_count
    capacity = 5 * tok_rows * top_count // (4 * experts)
    half = tok_rows // 2
    far = col_count // 2
    row = lax.axis_index("row")
    col = lax.axis_index("col")

    meta = jnp.concatenate([routes.astype(F32).T, gate_values.T], axis=0)
    metas = lax.all_gather(meta, "col", axis=0, tiled=False)

    chunks = {0: tokens}
    right, left = tokens, tokens
    for step in range(1, far):
        right = lax.ppermute(right, "col", ring(col_count, 1))
        left = lax.ppermute(left, "col", ring(col_count, -1))
        chunks[step], chunks[-step] = right, left
    right = lax.ppermute(right[:half], "col", ring(col_count, 1))
    left = lax.ppermute(left[half:], "col", ring(col_count, -1))
    chunks[far] = jnp.concatenate([right, left], axis=0)

    order = jnp.arange(tok_rows, dtype=jnp.int32)
    earlier = (order[:, None] < order[None, :]).astype(BF16)
    wanted = jnp.stack([(row ^ k) * col_count + col for k in range(row_count)]).astype(F32)
    slot_ids = jnp.arange(capacity, dtype=jnp.int32).astype(F32)

    def tables(offset):
        mine = lax.dynamic_index_in_dim(metas, (col - offset) % col_count, 0, keepdims=False)
        ids, gates = mine[:top_count], mine[top_count:]
        hit = ids[None, :, :] == wanted[:, None, None]
        named = jnp.any(hit, axis=1)
        gate = jnp.sum(jnp.where(hit, gates[None], 0.0), axis=1)
        before = jnp.dot(named.astype(BF16), earlier, preferred_element_type=F32)
        slot = jnp.where(named, before, -1.0)
        return slot, gate

    groups = [(0,)] + [(s, -s) for s in range(1, far)] + [(far,)]
    slots, gates_of = {}, {}
    for offset in [o for group in groups for o in group]:
        slots[offset], gates_of[offset] = tables(offset)

    w_gate, w_up, w_down = w_gate[0], w_up[0], w_down[0]
    returned = {}
    for group in groups:
        picks = []
        for offset in group:
            onehot = (slots[offset][:, None, :] == slot_ids[None, :, None]).astype(BF16)
            picked = jnp.dot(
                onehot.reshape(row_count * capacity, tok_rows), chunks[offset], preferred_element_type=F32
            ).astype(BF16)
            picks.append(picked.reshape(row_count, capacity, features))
        blocks = []
        for k in range(row_count):
            block = jnp.concatenate([p[k] for p in picks], axis=0)
            blocks.append(block if k == 0 else lax.ppermute(block, "row", swap(row_count, k)))
        results = expert_rows(jnp.concatenate(blocks, axis=0), w_gate, w_up, w_down)
        results = results.reshape(row_count, len(group), capacity, features)
        backs = []
        for k in range(row_count):
            block = results[k].reshape(len(group) * capacity, features)
            back = block if k == 0 else lax.ppermute(block, "row", swap(row_count, k))
            backs.append(back.reshape(len(group), capacity, features))
        for index, offset in enumerate(group):
            returned[offset] = jnp.concatenate([b[index] for b in backs], axis=0)

    def partial(offset):
        slot, gate = slots[offset], gates_of[offset]
        weights = jnp.where(slot[:, None, :] == slot_ids[None, :, None], gate[:, None, :], 0.0)
        weights = weights.reshape(row_count * capacity, tok_rows)
        high = weights.astype(BF16)
        low = (weights - high.astype(F32)).astype(BF16)
        rows = returned[offset]
        contract = (((0,), (0,)), ((), ()))
        return lax.dot_general(high, rows, contract, preferred_element_type=F32) + lax.dot_general(
            low, rows, contract, preferred_element_type=F32
        )

    ends = partial(far)
    left = lax.ppermute(ends[:half].astype(BF16), "col", ring(col_count, -1))
    right = lax.ppermute(ends[half:].astype(BF16), "col", ring(col_count, 1))
    left = jnp.concatenate([left.astype(F32), jnp.zeros((tok_rows - half, features), F32)], axis=0)
    right = jnp.concatenate([jnp.zeros((half, features), F32), right.astype(F32)], axis=0)
    for step in range(far - 1, 0, -1):
        left = (partial(step) + left).astype(BF16)
        right = (partial(-step) + right).astype(BF16)
        left = lax.ppermute(left, "col", ring(col_count, -1)).astype(F32)
        right = lax.ppermute(right, "col", ring(col_count, 1)).astype(F32)
    return (partial(0) + left + right).astype(BF16)


def solution(mesh):
    placed = (
        P(("dp", "row", "col"), None),
        P(("dp", "row", "col"), None),
        P(("dp", "row", "col"), None),
        P(("row", "col"), None, None),
        P(("row", "col"), None, None),
        P(("row", "col"), None, None),
    )
    return jax.shard_map(
        body, mesh=mesh, in_specs=placed, out_specs=P(("dp", "row", "col"), None), check_vma=False
    )
```

```python
import functools

import jax
import jax.numpy as jnp
from jax import lax
from jax.experimental import pallas as pl
from jax.experimental.pallas import tpu as pltpu
from jax.sharding import PartitionSpec as P

F32 = jnp.float32
BF16 = jnp.bfloat16
LANES = 128
ABSENT = -4096.0
VMEM_BYTES = 48 * 1024 * 1024
ANY = pl.BlockSpec(memory_space=pl.ANY)


def params(*semantics):
    return pltpu.CompilerParams(dimension_semantics=semantics or None, vmem_limit_bytes=VMEM_BYTES)


def ring(count, step):
    return [(i, (i + step) % count) for i in range(count)]


def swap(count, mask):
    return [(i, i ^ mask) for i in range(count)]


def prep_kernel(tokens_ref, routes_ref, gates_ref, out_ref, *, experts):
    rows, features = tokens_ref.shape
    top = routes_ref.shape[1]
    out_ref[:, :features] = tokens_ref[...]
    lane = lax.broadcasted_iota(jnp.int32, (rows, LANES), 1)
    expert = lane % experts
    named = jnp.zeros((rows, LANES), F32)
    gate = jnp.zeros((rows, LANES), F32)
    for k in range(top):
        hit = expert == routes_ref[:, k : k + 1]
        named = jnp.where(hit, 1.0, named)
        gate = jnp.where(hit, gates_ref[:, k : k + 1], gate)
    row_id = lax.broadcasted_iota(jnp.int32, (rows, rows), 0)
    col_id = lax.broadcasted_iota(jnp.int32, (rows, rows), 1)
    earlier = jnp.where(col_id < row_id, 1.0, 0.0).astype(BF16)
    before = jnp.dot(earlier, named.astype(BF16), preferred_element_type=F32)
    slot = jnp.where(named > 0.0, before, ABSENT)
    high = gate.astype(BF16).astype(F32)
    low = gate - high
    packed = jnp.where(lane < experts, slot, jnp.where(lane < 2 * experts, high, low))
    out_ref[:, features:] = packed.astype(BF16)


def prep(tokens, routes, gates, experts):
    rows, features = tokens.shape
    return pl.pallas_call(
        functools.partial(prep_kernel, experts=experts),
        out_shape=jax.ShapeDtypeStruct((rows, features + LANES), BF16),
        compiler_params=params(),
        name="prep",
    )(tokens, routes, gates)


def column(table, index):
    lane = lax.broadcasted_iota(jnp.int32, table.shape, 1)
    return jnp.sum(jnp.where(lane == index, table, 0.0), axis=1, keepdims=True)


def spread(columns, width, block):
    rows = columns[0].shape[0]
    lane = lax.broadcasted_iota(jnp.int32, (rows, width), 1)
    result = jnp.broadcast_to(columns[-1], (rows, width))
    for k in range(len(columns) - 2, -1, -1):
        result = jnp.where(lane < (k + 1) * block, columns[k], result)
    return result


def select_kernel(where_ref, *refs, n, mates, cols, capacity):
    data, metas, outs, hot_ref = refs[:n], refs[n : 2 * n], refs[-1 - mates : -1], refs[-1]
    width = mates * capacity

    @pl.when(pl.program_id(0) == 0)
    def _():
        for c in range(n):
            table = metas[c][...].astype(F32)
            rows = table.shape[0]
            slots = [column(table, (where_ref[0] ^ k) * cols + where_ref[1]) + k * capacity for k in range(mates)]
            lane = lax.broadcasted_iota(jnp.int32, (rows, width), 1).astype(F32)
            hot_ref[c] = jnp.where(spread(slots, width, capacity) == lane, 1.0, 0.0).astype(BF16)

    picked = [
        lax.dot_general(hot_ref[c], data[c][...], (((0,), (0,)), ((), ())), preferred_element_type=F32)
        for c in range(n)
    ]
    for k in range(mates):
        parts = [p[k * capacity : (k + 1) * capacity] for p in picked]
        outs[k][...] = (parts[0] if n == 1 else jnp.concatenate(parts, axis=0)).astype(BF16)


def select(where, chunks, after, mates, cols, capacity, tile=1024):
    n = len(chunks)
    rows, wide = chunks[0].shape
    features = wide - LANES
    data = pl.BlockSpec((rows, tile), lambda i, w: (0, i))
    meta = pl.BlockSpec((rows, LANES), lambda i, w: (0, features // LANES))
    out = pl.BlockSpec((n * capacity, tile), lambda i, w: (0, i))
    return pl.pallas_call(
        functools.partial(select_kernel, n=n, mates=mates, cols=cols, capacity=capacity),
        out_shape=[jax.ShapeDtypeStruct((n * capacity, features), BF16)] * mates,
        grid_spec=pltpu.PrefetchScalarGridSpec(
            num_scalar_prefetch=1,
            grid=(features // tile,),
            in_specs=[data] * n + [meta] * n + [ANY] * len(after),
            out_specs=[out] * mates,
            scratch_shapes=[pltpu.VMEM((n, rows, mates * capacity), BF16)],
        ),
        compiler_params=params("arbitrary"),
        name="select",
    )(where, *chunks, *chunks, *after)


def expert_kernel(*refs, mates):
    blocks, (gate_ref, up_ref, down_ref) = refs[:mates], refs[mates : mates + 3]
    outs, rows_ref, sum_ref = refs[-2 - mates : -2], refs[-2], refs[-1]
    step = pl.program_id(0)

    @pl.when(step == 0)
    def _():
        parts = [b[...].astype(F32) for b in blocks]
        rows_ref[...] = jnp.concatenate(parts, axis=0).astype(BF16)

    rows = rows_ref[...]
    gate_part = jnp.dot(rows, gate_ref[...], preferred_element_type=F32)
    up_part = jnp.dot(rows, up_ref[...], preferred_element_type=F32)
    hidden = (gate_part / (1.0 + jnp.exp(-gate_part)) * up_part).astype(BF16)
    part = jnp.dot(hidden, down_ref[...], preferred_element_type=F32)

    @pl.when(step == 0)
    def _():
        sum_ref[...] = part

    @pl.when(step > 0)
    def _():
        sum_ref[...] += part

    @pl.when(step == pl.num_programs(0) - 1)
    def _():
        size = outs[0].shape[0]
        for k in range(mates):
            outs[k][...] = sum_ref[k * size : (k + 1) * size].astype(BF16)


def expert(blocks, w_gate, w_up, w_down, after, tile=256):
    mates = len(blocks)
    size, features = blocks[0].shape
    hidden = w_gate.shape[2]
    block = pl.BlockSpec((size, features), lambda i: (0, 0))
    return pl.pallas_call(
        functools.partial(expert_kernel, mates=mates),
        out_shape=[jax.ShapeDtypeStruct((size, features), BF16)] * mates,
        grid=(hidden // tile,),
        in_specs=[block] * mates
        + [
            pl.BlockSpec((None, features, tile), lambda i: (0, 0, i)),
            pl.BlockSpec((None, features, tile), lambda i: (0, 0, i)),
            pl.BlockSpec((None, tile, features), lambda i: (0, i, 0)),
        ]
        + [ANY] * len(after),
        out_specs=[block] * mates,
        scratch_shapes=[
            pltpu.VMEM((mates * size, features), BF16),
            pltpu.VMEM((mates * size, features), F32),
        ],
        compiler_params=params("arbitrary"),
        name="expert",
    )(*blocks, w_gate, w_up, w_down, *after)


def combine_kernel(where_ref, *refs, n, mates, cols, capacity, experts, mode):
    blocks, metas = refs[:mates], refs[mates : mates + n]
    count = 0 if mode == "far" else 2
    adds = refs[mates + n : mates + n + count]
    heads = 1 if mode == "near" else 2
    outs, weight_ref = refs[-1 - heads : -1], refs[-1]
    width = mates * n * capacity
    tok = metas[0].shape[0]

    @pl.when(pl.program_id(0) == 0)
    def _():
        for c in range(n):
            table = metas[c][...].astype(F32)
            lane = lax.broadcasted_iota(jnp.int32, (tok, width), 1).astype(F32)
            slots, highs, lows = [], [], []
            for k in range(mates):
                index = (where_ref[0] ^ k) * cols + where_ref[1]
                slots.append(column(table, index) + (k * n + c) * capacity)
                highs.append(column(table, index + experts))
                lows.append(column(table, index + 2 * experts))
            hit = spread(slots, width, n * capacity) == lane
            weight_ref[c, :tok] = jnp.where(hit, spread(highs, width, n * capacity), 0.0).astype(BF16)
            weight_ref[c, tok:] = jnp.where(hit, spread(lows, width, n * capacity), 0.0).astype(BF16)

    rows = jnp.concatenate([b[...].astype(F32) for b in blocks], axis=0).astype(BF16)
    sums = []
    for c in range(n):
        both = jnp.dot(weight_ref[c], rows, preferred_element_type=F32)
        sums.append(both[:tok] + both[tok:])
    half = tok // 2
    if mode == "far":
        outs[0][...] = sums[0][:half].astype(BF16)
        outs[1][...] = sums[0][half:].astype(BF16)
    elif mode == "near":
        outs[0][...] = (sums[0] + adds[0][...].astype(F32) + adds[1][...].astype(F32)).astype(BF16)
    elif mode == "next":
        outs[0][:half] = (sums[0][:half] + adds[0][...].astype(F32)).astype(BF16)
        outs[0][half:] = sums[0][half:].astype(BF16)
        outs[1][:half] = sums[1][:half].astype(BF16)
        outs[1][half:] = (sums[1][half:] + adds[1][...].astype(F32)).astype(BF16)
    else:
        outs[0][...] = (sums[0] + adds[0][...].astype(F32)).astype(BF16)
        outs[1][...] = (sums[1] + adds[1][...].astype(F32)).astype(BF16)


def combine(where, blocks, chunks, adds, mode, after, cols, capacity, tile=1024):
    mates, n = len(blocks), len(chunks)
    rows, wide = chunks[0].shape
    features = wide - LANES
    heads = 1 if mode == "near" else 2
    out_rows = rows // 2 if mode == "far" else rows

    def spec(height):
        return pl.BlockSpec((height, tile), lambda i, w: (0, i))

    meta = pl.BlockSpec((rows, LANES), lambda i, w: (0, features // LANES))
    return pl.pallas_call(
        functools.partial(
            combine_kernel, n=n, mates=mates, cols=cols, capacity=capacity, experts=mates * cols, mode=mode
        ),
        out_shape=[jax.ShapeDtypeStruct((out_rows, features), BF16)] * heads,
        grid_spec=pltpu.PrefetchScalarGridSpec(
            num_scalar_prefetch=1,
            grid=(features // tile,),
            in_specs=[spec(n * capacity)] * mates
            + [meta] * n
            + [spec(a.shape[0]) for a in adds]
            + [ANY] * len(after),
            out_specs=[spec(out_rows)] * heads,
            scratch_shapes=[pltpu.VMEM((n, 2 * rows, mates * n * capacity), BF16)],
        ),
        compiler_params=params("arbitrary"),
        name="combine",
    )(where, *blocks, *chunks, *adds, *after)


def body(tokens, routes, gate_values, w_gate, w_up, w_down):
    tok_rows, features = tokens.shape
    top_count = routes.shape[1]
    mates = lax.axis_size("row")
    cols = lax.axis_size("col")
    experts = mates * cols
    capacity = 5 * tok_rows * top_count // (4 * experts)
    half = tok_rows // 2
    far = cols // 2
    where = jnp.stack([lax.axis_index("row"), lax.axis_index("col")]).astype(jnp.int32)

    def right(x):
        return lax.ppermute(x, "col", ring(cols, 1))

    def left(x):
        return lax.ppermute(x, "col", ring(cols, -1))

    def exchange(blocks):
        order = (2, 3, 1)
        moved = {k: lax.ppermute(blocks[k], "row", swap(mates, k)) for k in order}
        return [blocks[0]] + [moved[k] for k in range(1, mates)]

    last = []

    def pick(chunks):
        out = select(where, chunks, last[-1:], mates, cols, capacity)
        last.append(out[0])
        return exchange(out)

    def run(blocks):
        out = expert(blocks, w_gate, w_up, w_down, last[-1:])
        last.append(out[0])
        return out

    def merge(blocks, chunks, adds, mode):
        out = combine(where, blocks, chunks, adds, mode, last[-1:], cols, capacity)
        last.append(out[0])
        return out

    payload = prep(tokens, routes, gate_values, experts)
    chunk = {0: payload}
    for s in range(1, far):
        chunk[s], chunk[-s] = right(chunk[s - 1]), left(chunk[1 - s])
    chunk[far] = jnp.concatenate([right(chunk[far - 1][:half]), left(chunk[1 - far][half:])], axis=0)
    groups = [[chunk[0]]] + [[chunk[s], chunk[-s]] for s in range(1, far)] + [[chunk[far]]]

    arrived, done = {}, {}
    arrived[0] = pick(groups[0])
    arrived[1] = pick(groups[1])
    for s in range(2, far):
        done[s - 2] = run(arrived[s - 2])
        arrived[s] = pick(groups[s])
    arrived[far] = pick(groups[far])
    for s in range(far - 2, far + 1):
        done[s] = run(arrived[s])

    back = {far: exchange(done[far]), far - 1: exchange(done[far - 1])}

    def gated(s, gate):
        held = lax.optimization_barrier((*done[s], *gate))
        return exchange(list(held[:mates]))

    for s in range(far - 2, -1, -1):
        back[s] = gated(s, back[s + 2])

    to_left, to_right = merge(back[far], groups[far], [], "far")
    for s in range(far - 1, 0, -1):
        adds = [left(to_left), right(to_right)]
        to_left, to_right = merge(back[s], groups[s], adds, "next" if s == far - 1 else "mid")
    return merge(back[0], groups[0], [left(to_left), right(to_right)], "near")[0]


def solution(mesh):
    placed = (
        P(("dp", "row", "col"), None),
        P(("dp", "row", "col"), None),
        P(("dp", "row", "col"), None),
        P(("row", "col"), None, None),
        P(("row", "col"), None, None),
        P(("row", "col"), None, None),
    )
    return jax.shard_map(
        body, mesh=mesh, in_specs=placed, out_specs=P(("dp", "row", "col"), None), check_vma=False
    )
```

```python
import functools

import jax
import jax.numpy as jnp
from jax import lax
from jax.experimental import pallas as pl
from jax.experimental.pallas import tpu as pltpu
from jax.sharding import PartitionSpec as P

F32 = jnp.float32
BF16 = jnp.bfloat16
LANES = 128
ABSENT = -4096.0
VMEM_BYTES = 24 * 1024 * 1024
ANY = pl.BlockSpec(memory_space=pl.ANY)
LIGHT = pl.CostEstimate(flops=1, transcendentals=0, bytes_accessed=1)


def params(*semantics):
    return pltpu.CompilerParams(dimension_semantics=semantics or None, vmem_limit_bytes=VMEM_BYTES)


def ring(count, step):
    return [(i, (i + step) % count) for i in range(count)]


def swap(count, mask):
    return [(i, i ^ mask) for i in range(count)]


def prep_kernel(tokens_ref, routes_in, gates_in, out_ref, routes_ref, gates_ref, table_ref, sems, *, experts):
    rows, features = tokens_ref.shape
    top = routes_in.shape[0]
    routes_copy = pltpu.make_async_copy(routes_in, routes_ref, sems.at[2])
    gates_copy = pltpu.make_async_copy(gates_in, gates_ref, sems.at[3])
    routes_copy.start()
    gates_copy.start()
    body_copy = pltpu.make_async_copy(tokens_ref, out_ref.at[:, pl.ds(0, features)], sems.at[0])
    body_copy.start()
    routes_copy.wait()
    gates_copy.wait()
    line = lax.broadcasted_iota(jnp.int32, (LANES, rows), 0)
    expert = line % experts
    named = jnp.zeros((LANES, rows), F32)
    gate = jnp.zeros((LANES, rows), F32)
    for k in range(top):
        hit = expert == routes_ref[k : k + 1, :]
        named = jnp.where(hit, 1.0, named)
        gate = jnp.where(hit, gates_ref[k : k + 1, :], gate)
    row_id = lax.broadcasted_iota(jnp.int32, (rows, rows), 0)
    col_id = lax.broadcasted_iota(jnp.int32, (rows, rows), 1)
    earlier = jnp.where(row_id < col_id, 1.0, 0.0).astype(BF16)
    before = jnp.dot(named.astype(BF16), earlier, preferred_element_type=F32)
    slot = jnp.where(named > 0.0, before, ABSENT)
    high = gate.astype(BF16).astype(F32)
    packed = jnp.where(line < experts, slot, jnp.where(line < 2 * experts, high, gate - high))
    table_ref[...] = jnp.transpose(packed).astype(BF16)
    table_copy = pltpu.make_async_copy(table_ref, out_ref.at[:, pl.ds(features, LANES)], sems.at[1])
    table_copy.start()
    body_copy.wait()
    table_copy.wait()


def prep(tokens, routes, gates, experts):
    rows, features = tokens.shape
    far_side = pl.BlockSpec(memory_space=pltpu.HBM)
    top = routes.shape[1]
    return pl.pallas_call(
        functools.partial(prep_kernel, experts=experts),
        out_shape=jax.ShapeDtypeStruct((rows, features + LANES), BF16),
        in_specs=[far_side] * 3,
        out_specs=far_side,
        scratch_shapes=[
            pltpu.VMEM((top, rows), jnp.int32),
            pltpu.VMEM((top, rows), F32),
            pltpu.VMEM((rows, LANES), BF16),
            pltpu.SemaphoreType.DMA((4,)),
        ],
        compiler_params=params(),
        cost_estimate=LIGHT,
        name="prep",
    )(tokens, routes.T, gates.T)


def column(table, index):
    lane = lax.broadcasted_iota(jnp.int32, table.shape, 1)
    return jnp.sum(jnp.where(lane == index, table, 0.0), axis=1, keepdims=True)


def spread(columns, width, block):
    rows = columns[0].shape[0]
    lane = lax.broadcasted_iota(jnp.int32, (rows, width), 1)
    result = jnp.broadcast_to(columns[-1], (rows, width))
    for k in range(len(columns) - 2, -1, -1):
        result = jnp.where(lane < (k + 1) * block, columns[k], result)
    return result


def near_height(size):
    return size if size % 16 == 0 else 2 * size


def stacked(refs):
    return refs[0][...] if len(refs) == 1 else jnp.concatenate([r[...] for r in refs], axis=0)


def select_kernel(where_ref, *refs, n, mates, cols, capacity):
    data = [refs[:2]] if n == 0 else [(r,) for r in refs[:n]]
    metas = [refs[2:4]] if n == 0 else [(r,) for r in refs[n : 2 * n]]
    n = len(data)
    own_ref, core_ref, cross_ref, hot_ref = refs[-4:]
    width = mates * capacity

    @pl.when(pl.program_id(0) == 0)
    def _():
        for c in range(n):
            table = stacked(metas[c]).astype(F32)
            rows = table.shape[0]
            slots = [column(table, (where_ref[0] ^ k) * cols + where_ref[1]) + k * capacity for k in range(mates)]
            lane = lax.broadcasted_iota(jnp.int32, (rows, width), 1).astype(F32)
            hot_ref[c] = jnp.where(spread(slots, width, capacity) == lane, 1.0, 0.0).astype(BF16)

    picked = [
        lax.dot_general(hot_ref[c], stacked(data[c]), (((0,), (0,)), ((), ())), preferred_element_type=F32)
        for c in range(n)
    ]

    def rows_for(ks):
        parts = [p[k * capacity : (k + 1) * capacity] for k in ks for p in picked]
        return (parts[0] if len(parts) == 1 else jnp.concatenate(parts, axis=0)).astype(BF16)

    own_ref[...] = rows_for((0,))
    core_ref[...] = rows_for((1,))
    cross_ref[...] = rows_for((2, 3))


def select(where, chunks, after, mates, cols, capacity, tokens, tile=1024):
    rows, wide = chunks[0].shape
    pieces = len(chunks)
    halves = pieces == 2 and rows < tokens
    n = 1 if halves else pieces
    features = wide - LANES
    size = n * capacity
    data = pl.BlockSpec((rows, tile), lambda i, w: (0, i))
    meta = pl.BlockSpec((rows, LANES), lambda i, w: (0, features // LANES))
    heights = (size, size, 2 * size)
    return pl.pallas_call(
        functools.partial(select_kernel, n=0 if halves else n, mates=mates, cols=cols, capacity=capacity),
        out_shape=[jax.ShapeDtypeStruct((h, features), BF16) for h in heights],
        grid_spec=pltpu.PrefetchScalarGridSpec(
            num_scalar_prefetch=1,
            grid=(features // tile,),
            in_specs=[data] * pieces + [meta] * pieces + [ANY] * len(after),
            out_specs=[pl.BlockSpec((h, tile), lambda i, w: (0, i)) for h in heights],
            scratch_shapes=[pltpu.VMEM((n, tokens, mates * capacity), BF16)],
        ),
        compiler_params=params("arbitrary"),
        cost_estimate=LIGHT,
        name="select",
    )(where, *chunks, *chunks, *after)


def expert_kernel(own_in, core_in, cross_in, gate_ref, up_ref, down_ref, *refs):
    own_out, core_out, cross_out = refs[-3:]
    size = own_in.shape[0]
    parts = [own_in[...].astype(F32), core_in[...].astype(F32), cross_in[...].astype(F32)[:size]]
    rows = jnp.concatenate(parts, axis=0).astype(BF16)
    gate_part = jnp.dot(rows, gate_ref[0], preferred_element_type=F32)
    up_part = jnp.dot(rows, up_ref[0], preferred_element_type=F32)
    hidden = (gate_part / (1.0 + jnp.exp(-gate_part)) * up_part).astype(BF16)
    result = jnp.dot(hidden, down_ref[0], preferred_element_type=F32)
    own_out[...] = result[:size].astype(BF16)
    core_out[...] = result[size : 2 * size].astype(BF16)
    crossing = jnp.concatenate([result[3 * size :], result[2 * size : 3 * size]], axis=0)
    cross_out[...] = crossing.astype(BF16)


def expert(arrivals, w_gate, w_up, w_down, after):
    size, features = arrivals[0].shape

    def whole(height):
        return pl.BlockSpec((height, features), lambda i: (0, 0))

    heights = (size, size, 2 * size)
    return pl.pallas_call(
        expert_kernel,
        out_shape=[jax.ShapeDtypeStruct((h, features), BF16) for h in heights],
        grid=(1,),
        in_specs=[whole(size), whole(2 * size), whole(near_height(size))]
        + [pl.BlockSpec(memory_space=pltpu.VMEM)] * 3
        + [ANY] * len(after),
        out_specs=[whole(h) for h in heights],
        compiler_params=params("arbitrary"),
        cost_estimate=LIGHT,
        name="expert",
    )(*arrivals, w_gate, w_up, w_down, *after)


def weigh_kernel(where_ref, *refs, n, cols, capacity, experts, order):
    pieces = 2 if n == 0 else n
    blocks, metas = refs[:4], refs[4 : 4 + pieces]
    metas = [metas] if n == 0 else [(m,) for m in metas]
    n = heads = len(metas)
    outs, weight_ref = refs[-1 - heads : -1], refs[-1]
    block = n * capacity
    width = len(order) * block
    tok = weight_ref.shape[1] // 2

    @pl.when(pl.program_id(0) == 0)
    def _():
        for c in range(n):
            table = stacked(metas[c]).astype(F32)
            lane = lax.broadcasted_iota(jnp.int32, (tok, width), 1).astype(F32)
            slots, highs, lows = [], [], []
            for place, k in enumerate(order):
                index = (where_ref[0] ^ k) * cols + where_ref[1]
                slots.append(column(table, index) + (place * n + c) * capacity)
                highs.append(column(table, index + experts))
                lows.append(column(table, index + 2 * experts))
            hit = spread(slots, width, block) == lane
            weight_ref[c, :tok] = jnp.where(hit, spread(highs, width, block), 0.0).astype(BF16)
            weight_ref[c, tok:] = jnp.where(hit, spread(lows, width, block), 0.0).astype(BF16)

    rows = jnp.concatenate([b[...].astype(F32)[:block] for b in blocks], axis=0).astype(BF16)
    for c in range(heads):
        both = jnp.dot(weight_ref[c], rows, preferred_element_type=F32)
        outs[c][...] = (both[:tok] + both[tok:]).astype(outs[c].dtype)


def weigh(where, blocks, chunks, dtype, after, mates, cols, capacity, tokens, tile=1024):
    height, wide = chunks[0].shape
    rows, pieces = tokens, len(chunks)
    halves = pieces == 2 and height < tokens
    n = 1 if halves else pieces
    features = wide - LANES
    size = n * capacity

    def spec(height):
        return pl.BlockSpec((height, tile), lambda i, w: (0, i))

    meta = pl.BlockSpec((height, LANES), lambda i, w: (0, features // LANES))
    return pl.pallas_call(
        functools.partial(
            weigh_kernel,
            n=0 if halves else n,
            cols=cols,
            capacity=capacity,
            experts=mates * cols,
            order=(0, 1, 3, 2),
        ),
        out_shape=[jax.ShapeDtypeStruct((rows, features), dtype)] * n,
        grid_spec=pltpu.PrefetchScalarGridSpec(
            num_scalar_prefetch=1,
            grid=(features // tile,),
            in_specs=[spec(size)] * (mates - 1)
            + [spec(near_height(size))]
            + [meta] * pieces
            + [ANY] * len(after),
            out_specs=[spec(rows)] * n,
            scratch_shapes=[pltpu.VMEM((n, 2 * rows, mates * size), BF16)],
        ),
        compiler_params=params("arbitrary"),
        cost_estimate=LIGHT,
        name="weigh",
    )(where, *blocks, *chunks, *after)


def add_kernel(*refs, heads, added):
    sums, adds, outs = refs[:heads], refs[heads : heads + len(added)], refs[-heads:]
    for c in range(heads):
        total = sums[c][...]
        for add, head in zip(adds, added):
            if head == c:
                total = total + add[...].astype(F32)
        outs[c][...] = total.astype(BF16)


def add_ring(sums, adds, added, tile=1024):
    heads = len(sums)
    rows, features = sums[0].shape
    spec = pl.BlockSpec((rows, tile), lambda i: (0, i))
    return pl.pallas_call(
        functools.partial(add_kernel, heads=heads, added=added),
        out_shape=[jax.ShapeDtypeStruct((rows, features), BF16)] * heads,
        grid=(features // tile,),
        in_specs=[spec] * (heads + len(adds)),
        out_specs=[spec] * heads,
        compiler_params=params("arbitrary"),
        cost_estimate=LIGHT,
        name="add_ring",
    )(*sums, *adds)


def body(tokens, routes, gate_values, w_gate, w_up, w_down):
    tok_rows = tokens.shape[0]
    top_count = routes.shape[1]
    mates = lax.axis_size("row")
    cols = lax.axis_size("col")
    experts = mates * cols
    capacity = 5 * tok_rows * top_count // (4 * experts)
    far = cols // 2
    half = tok_rows // 2
    where = jnp.stack([lax.axis_index("row"), lax.axis_index("col")]).astype(jnp.int32)

    def right(x):
        return lax.ppermute(x, "col", ring(cols, 1))

    def left(x):
        return lax.ppermute(x, "col", ring(cols, -1))

    def over_chip(cross):
        return lax.ppermute(cross, "row", swap(mates, 2))

    def gathered(own, core, crossed):
        size = core.shape[0]
        passed_on = lax.ppermute(crossed[size:], "row", swap(mates, 1))
        return own, lax.ppermute(core, "row", swap(mates, 1)), passed_on, crossed

    last = []

    def pick(chunks):
        own, core, cross = select(where, chunks, last[-1:], mates, cols, capacity, tok_rows)
        last.append(own)
        return own, core, over_chip(cross)

    def settle(own, core, crossed):
        both = jnp.concatenate([core, crossed[core.shape[0] :]], axis=0)
        return own, lax.ppermute(both, "row", swap(mates, 1)), crossed

    def run(arrivals):
        out = expert(arrivals, w_gate, w_up, w_down, last[-1:])
        last.append(out[0])
        return out

    def merge(blocks, chunks, adds, added):
        out = weigh(
            where, blocks, chunks, F32 if adds else BF16, last[-1:], mates, cols, capacity, tok_rows
        )
        if adds:
            out = add_ring(out, adds, added)
        last.append(out[0])
        return out

    payload = prep(tokens, routes, gate_values, experts)
    groups, arrived, done = [[payload]], {}, {}
    to_right, to_left = right(payload), left(payload)
    arrived[0] = pick(groups[0])
    for s in range(1, far):
        gate = arrived[0][2] if s == 1 else last[-1]
        from_left, from_right, unused = lax.optimization_barrier((to_right, to_left, gate))
        groups.append([from_left, from_right])
        if s < far - 1:
            to_right, to_left = right(from_left), left(from_right)
        else:
            to_right, to_left = right(from_left[:half]), left(from_right[half:])
        arrived[s] = pick(groups[s])
        if s > 1:
            done[s - 2] = run(settle(*arrived[s - 2]))
    groups.append([to_right, to_left])
    arrived[far] = pick(groups[far])
    done[far - 2] = run(settle(*arrived[far - 2]))
    for s in (far, far - 1):
        own, core, crossed = arrived[s]
        crossed, unused = lax.optimization_barrier((crossed, done[far - 2][0]))
        done[s] = run(settle(own, core, crossed))

    crossed = {far: over_chip(done[far][2])}
    held, unused = lax.optimization_barrier((done[far - 1][2], crossed[far]))
    crossed[far - 1] = over_chip(held)
    adds, added = [], ()
    for s in range(far, 0, -1):
        sums = merge(gathered(*done[s][:2], crossed[s]), groups[s], adds, added)
        if s > 1:
            held, unused = lax.optimization_barrier((done[s - 2][2], sums[0]))
            crossed[s - 2] = over_chip(held)
        adds, added = [left(sums[0])], (0,)
        if len(sums) > 1:
            adds, added = adds + [right(sums[1])], (0, 1)
    [combined] = merge(gathered(*done[0][:2], crossed[0]), groups[0], adds, (0, 0))
    return combined


def solution(mesh):
    placed = (
        P(("dp", "row", "col"), None),
        P(("dp", "row", "col"), None),
        P(("dp", "row", "col"), None),
        P(("row", "col"), None, None),
        P(("row", "col"), None, None),
        P(("row", "col"), None, None),
    )
    return jax.shard_map(
        body, mesh=mesh, in_specs=placed, out_specs=P(("dp", "row", "col"), None), check_vma=False
    )
```

```python
import functools

import jax
import jax.numpy as jnp
from jax import lax
from jax.experimental import pallas as pl
from jax.experimental.pallas import tpu as pltpu
from jax.sharding import PartitionSpec as P

F32 = jnp.float32
BF16 = jnp.bfloat16
LANES = 128
ABSENT = -4096.0
VMEM_BYTES = 24 * 1024 * 1024
ANY = pl.BlockSpec(memory_space=pl.ANY)
LIGHT = pl.CostEstimate(flops=1, transcendentals=0, bytes_accessed=1)


def params(*semantics):
    return pltpu.CompilerParams(dimension_semantics=semantics or None, vmem_limit_bytes=VMEM_BYTES)


def ring(count, step):
    return [(i, (i + step) % count) for i in range(count)]


def swap(count, mask):
    return [(i, i ^ mask) for i in range(count)]


def prep_kernel(tokens_ref, routes_in, gates_in, out_ref, routes_ref, gates_ref, table_ref, sems, *, experts):
    rows, features = tokens_ref.shape
    top = routes_in.shape[0]
    routes_copy = pltpu.make_async_copy(routes_in, routes_ref, sems.at[2])
    gates_copy = pltpu.make_async_copy(gates_in, gates_ref, sems.at[3])
    routes_copy.start()
    gates_copy.start()
    body_copy = pltpu.make_async_copy(tokens_ref, out_ref.at[:, pl.ds(0, features)], sems.at[0])
    body_copy.start()
    routes_copy.wait()
    gates_copy.wait()
    line = lax.broadcasted_iota(jnp.int32, (LANES, rows), 0)
    expert = line % experts
    named = jnp.zeros((LANES, rows), F32)
    gate = jnp.zeros((LANES, rows), F32)
    for k in range(top):
        hit = expert == routes_ref[k : k + 1, :]
        named = jnp.where(hit, 1.0, named)
        gate = jnp.where(hit, gates_ref[k : k + 1, :], gate)
    row_id = lax.broadcasted_iota(jnp.int32, (rows, rows), 0)
    col_id = lax.broadcasted_iota(jnp.int32, (rows, rows), 1)
    earlier = jnp.where(row_id < col_id, 1.0, 0.0).astype(BF16)
    before = jnp.dot(named.astype(BF16), earlier, preferred_element_type=F32)
    slot = jnp.where(named > 0.0, before, ABSENT)
    high = gate.astype(BF16).astype(F32)
    packed = jnp.where(line < experts, slot, jnp.where(line < 2 * experts, high, gate - high))
    table_ref[...] = jnp.transpose(packed).astype(BF16)
    table_copy = pltpu.make_async_copy(table_ref, out_ref.at[:, pl.ds(features, LANES)], sems.at[1])
    table_copy.start()
    body_copy.wait()
    table_copy.wait()


def prep(tokens, routes, gates, experts):
    rows, features = tokens.shape
    far_side = pl.BlockSpec(memory_space=pltpu.HBM)
    top = routes.shape[1]
    return pl.pallas_call(
        functools.partial(prep_kernel, experts=experts),
        out_shape=jax.ShapeDtypeStruct((rows, features + LANES), BF16),
        in_specs=[far_side] * 3,
        out_specs=far_side,
        scratch_shapes=[
            pltpu.VMEM((top, rows), jnp.int32),
            pltpu.VMEM((top, rows), F32),
            pltpu.VMEM((rows, LANES), BF16),
            pltpu.SemaphoreType.DMA((4,)),
        ],
        compiler_params=params(),
        cost_estimate=LIGHT,
        name="prep",
    )(*[pltpu.with_memory_space_constraint(x, pltpu.HBM) for x in (tokens, routes.T, gates.T)])


def column(table, index):
    lane = lax.broadcasted_iota(jnp.int32, table.shape, 1)
    return jnp.sum(jnp.where(lane == index, table, 0.0), axis=1, keepdims=True)


def spread(columns, width, block):
    rows = columns[0].shape[0]
    lane = lax.broadcasted_iota(jnp.int32, (rows, width), 1)
    result = jnp.broadcast_to(columns[-1], (rows, width))
    for k in range(len(columns) - 2, -1, -1):
        result = jnp.where(lane < (k + 1) * block, columns[k], result)
    return result


def near_height(size):
    return size if size % 16 == 0 else 2 * size


def stacked(refs):
    return refs[0][...] if len(refs) == 1 else jnp.concatenate([r[...] for r in refs], axis=0)


def select_kernel(where_ref, *refs, n, mates, cols, capacity):
    data = [refs[:2]] if n == 0 else [(r,) for r in refs[:n]]
    metas = [refs[2:4]] if n == 0 else [(r,) for r in refs[n : 2 * n]]
    n = len(data)
    own_ref, core_ref, cross_ref, hot_ref = refs[-4:]
    width = mates * capacity

    @pl.when(pl.program_id(0) == 0)
    def _():
        for c in range(n):
            table = stacked(metas[c]).astype(F32)
            rows = table.shape[0]
            slots = [column(table, (where_ref[0] ^ k) * cols + where_ref[1]) + k * capacity for k in range(mates)]
            lane = lax.broadcasted_iota(jnp.int32, (rows, width), 1).astype(F32)
            hot_ref[c] = jnp.where(spread(slots, width, capacity) == lane, 1.0, 0.0).astype(BF16)

    picked = [
        lax.dot_general(hot_ref[c], stacked(data[c]), (((0,), (0,)), ((), ())), preferred_element_type=F32)
        for c in range(n)
    ]

    def rows_for(ks):
        parts = [p[k * capacity : (k + 1) * capacity] for k in ks for p in picked]
        return (parts[0] if len(parts) == 1 else jnp.concatenate(parts, axis=0)).astype(BF16)

    own_ref[...] = rows_for((0,))
    core_ref[...] = rows_for((1,))
    cross_ref[...] = rows_for((2, 3))


def select(where, chunks, after, mates, cols, capacity, tokens, tile=1024):
    rows, wide = chunks[0].shape
    pieces = len(chunks)
    halves = pieces == 2 and rows < tokens
    n = 1 if halves else pieces
    features = wide - LANES
    size = n * capacity
    data = pl.BlockSpec((rows, tile), lambda i, w: (0, i))
    meta = pl.BlockSpec((rows, LANES), lambda i, w: (0, features // LANES))
    heights = (size, size, 2 * size)
    return pl.pallas_call(
        functools.partial(select_kernel, n=0 if halves else n, mates=mates, cols=cols, capacity=capacity),
        out_shape=[jax.ShapeDtypeStruct((h, features), BF16) for h in heights],
        grid_spec=pltpu.PrefetchScalarGridSpec(
            num_scalar_prefetch=1,
            grid=(features // tile,),
            in_specs=[data] * pieces + [meta] * pieces + [ANY] * len(after),
            out_specs=[pl.BlockSpec((h, tile), lambda i, w: (0, i)) for h in heights],
            scratch_shapes=[pltpu.VMEM((n, tokens, mates * capacity), BF16)],
        ),
        compiler_params=params("arbitrary"),
        cost_estimate=LIGHT,
        name="select",
    )(where, *chunks, *chunks, *after)


def expert_kernel(own_in, core_in, cross_in, gate_ref, up_ref, down_ref, *refs):
    own_out, core_out, cross_out = refs[-3:]
    size = own_in.shape[0]
    parts = [own_in[...].astype(F32), core_in[...].astype(F32), cross_in[...].astype(F32)[:size]]
    rows = jnp.concatenate(parts, axis=0).astype(BF16)
    gate_part = jnp.dot(rows, gate_ref[0], preferred_element_type=F32)
    up_part = jnp.dot(rows, up_ref[0], preferred_element_type=F32)
    hidden = (gate_part / (1.0 + jnp.exp(-gate_part)) * up_part).astype(BF16)
    result = jnp.dot(hidden, down_ref[0], preferred_element_type=F32)
    own_out[...] = result[:size].astype(BF16)
    core_out[...] = result[size : 2 * size].astype(BF16)
    crossing = jnp.concatenate([result[3 * size :], result[2 * size : 3 * size]], axis=0)
    cross_out[...] = crossing.astype(BF16)


def expert(arrivals, w_gate, w_up, w_down, after):
    size, features = arrivals[0].shape

    def whole(height):
        return pl.BlockSpec((height, features), lambda i: (0, 0))

    heights = (size, size, 2 * size)
    return pl.pallas_call(
        expert_kernel,
        out_shape=[jax.ShapeDtypeStruct((h, features), BF16) for h in heights],
        grid=(1,),
        in_specs=[whole(size), whole(2 * size), whole(near_height(size))]
        + [pl.BlockSpec(memory_space=pltpu.VMEM)] * 3
        + [ANY] * len(after),
        out_specs=[whole(h) for h in heights],
        compiler_params=params("arbitrary"),
        cost_estimate=LIGHT,
        name="expert",
    )(*arrivals, w_gate, w_up, w_down, *after)


def weigh_kernel(where_ref, *refs, n, cols, capacity, experts, order):
    pieces = 2 if n == 0 else n
    blocks, metas = refs[:4], refs[4 : 4 + pieces]
    metas = [metas] if n == 0 else [(m,) for m in metas]
    n = heads = len(metas)
    outs, weight_ref = refs[-1 - heads : -1], refs[-1]
    block = n * capacity
    width = len(order) * block
    tok = weight_ref.shape[1] // 2

    @pl.when(pl.program_id(0) == 0)
    def _():
        for c in range(n):
            table = stacked(metas[c]).astype(F32)
            lane = lax.broadcasted_iota(jnp.int32, (tok, width), 1).astype(F32)
            slots, highs, lows = [], [], []
            for place, k in enumerate(order):
                index = (where_ref[0] ^ k) * cols + where_ref[1]
                slots.append(column(table, index) + (place * n + c) * capacity)
                highs.append(column(table, index + experts))
                lows.append(column(table, index + 2 * experts))
            hit = spread(slots, width, block) == lane
            weight_ref[c, :tok] = jnp.where(hit, spread(highs, width, block), 0.0).astype(BF16)
            weight_ref[c, tok:] = jnp.where(hit, spread(lows, width, block), 0.0).astype(BF16)

    rows = jnp.concatenate([b[...].astype(F32)[:block] for b in blocks], axis=0).astype(BF16)
    for c in range(heads):
        both = jnp.dot(weight_ref[c], rows, preferred_element_type=F32)
        outs[c][...] = (both[:tok] + both[tok:]).astype(outs[c].dtype)


def weigh(where, blocks, chunks, dtype, after, mates, cols, capacity, tokens, tile=1024):
    height, wide = chunks[0].shape
    rows, pieces = tokens, len(chunks)
    halves = pieces == 2 and height < tokens
    n = 1 if halves else pieces
    features = wide - LANES
    size = n * capacity

    def spec(height):
        return pl.BlockSpec((height, tile), lambda i, w: (0, i))

    meta = pl.BlockSpec((height, LANES), lambda i, w: (0, features // LANES))
    return pl.pallas_call(
        functools.partial(
            weigh_kernel,
            n=0 if halves else n,
            cols=cols,
            capacity=capacity,
            experts=mates * cols,
            order=(0, 1, 3, 2),
        ),
        out_shape=[jax.ShapeDtypeStruct((rows, features), dtype)] * n,
        grid_spec=pltpu.PrefetchScalarGridSpec(
            num_scalar_prefetch=1,
            grid=(features // tile,),
            in_specs=[spec(size)] * (mates - 1)
            + [spec(near_height(size))]
            + [meta] * pieces
            + [ANY] * len(after),
            out_specs=[spec(rows)] * n,
            scratch_shapes=[pltpu.VMEM((n, 2 * rows, mates * size), BF16)],
        ),
        compiler_params=params("arbitrary"),
        cost_estimate=LIGHT,
        name="weigh",
    )(where, *blocks, *chunks, *after)


def add_kernel(*refs, heads, added):
    sums, adds, outs = refs[:heads], refs[heads : heads + len(added)], refs[-heads:]
    for c in range(heads):
        total = sums[c][...]
        for add, head in zip(adds, added):
            if head == c:
                total = total + add[...].astype(F32)
        outs[c][...] = total.astype(BF16)


def add_ring(sums, adds, added, tile=1024):
    heads = len(sums)
    rows, features = sums[0].shape
    spec = pl.BlockSpec((rows, tile), lambda i: (0, i))
    return pl.pallas_call(
        functools.partial(add_kernel, heads=heads, added=added),
        out_shape=[jax.ShapeDtypeStruct((rows, features), BF16)] * heads,
        grid=(features // tile,),
        in_specs=[spec] * (heads + len(adds)),
        out_specs=[spec] * heads,
        compiler_params=params("arbitrary"),
        cost_estimate=LIGHT,
        name="add_ring",
    )(*sums, *adds)


def body(tokens, routes, gate_values, w_gate, w_up, w_down):
    tok_rows = tokens.shape[0]
    top_count = routes.shape[1]
    mates = lax.axis_size("row")
    cols = lax.axis_size("col")
    experts = mates * cols
    capacity = 5 * tok_rows * top_count // (4 * experts)
    far = cols // 2
    half = tok_rows // 2
    where = jnp.stack([lax.axis_index("row"), lax.axis_index("col")]).astype(jnp.int32)

    def right(x):
        return lax.ppermute(x, "col", ring(cols, 1))

    def left(x):
        return lax.ppermute(x, "col", ring(cols, -1))

    def over_chip(cross):
        return lax.ppermute(cross, "row", swap(mates, 2))

    def gathered(own, core, crossed):
        size = core.shape[0]
        passed_on = lax.ppermute(crossed[size:], "row", swap(mates, 1))
        return own, lax.ppermute(core, "row", swap(mates, 1)), passed_on, crossed

    last = []

    def pick(chunks):
        own, core, cross = select(where, chunks, last[-1:], mates, cols, capacity, tok_rows)
        last.append(own)
        return own, core, over_chip(cross)

    def settle(own, core, crossed, gate=None):
        if gate is not None:
            crossed, unused = lax.optimization_barrier((crossed, gate))
        both = jnp.concatenate([core, crossed[core.shape[0] :]], axis=0)
        return own, lax.ppermute(both, "row", swap(mates, 1)), crossed

    def run(arrivals):
        out = expert(arrivals, w_gate, w_up, w_down, last[-1:])
        last.append(out[0])
        return out

    def merge(blocks, chunks, adds, added):
        out = weigh(
            where, blocks, chunks, F32 if adds else BF16, last[-1:], mates, cols, capacity, tok_rows
        )
        if adds:
            out = add_ring(out, adds, added)
        last.append(out[0])
        return out

    payload = prep(tokens, routes, gate_values, experts)
    groups, arrived, done = [[payload]], {}, {}
    to_right, to_left = right(payload), left(payload)
    arrived[0] = pick(groups[0])
    for s in range(1, far):
        gate = arrived[0][2] if s == 1 else last[-1]
        from_left, from_right, unused = lax.optimization_barrier((to_right, to_left, gate))
        groups.append([from_left, from_right])
        if s < far - 1:
            to_right, to_left = right(from_left), left(from_right)
        else:
            to_right, to_left = right(from_left[:half]), left(from_right[half:])
        arrived[s] = pick(groups[s])
        if s == far - 1:
            arrived[s - 1] = settle(*arrived[s - 1], last[-1])
        if s == far - 1:
            for early in range(far - 2):
                done[early] = run(settle(*arrived[early]))
    groups.append([to_right, to_left])
    arrived[far] = pick(groups[far])
    done[far - 2] = run(arrived[far - 2])
    for s in (far, far - 1):
        own, core, crossed = arrived[s]
        crossed, unused = lax.optimization_barrier((crossed, done[far - 2][0]))
        done[s] = run(settle(own, core, crossed))

    crossed = {far: over_chip(done[far][2])}
    held, unused = lax.optimization_barrier((done[far - 1][2], crossed[far]))
    crossed[far - 1] = over_chip(held)
    adds, added = [], ()
    for s in range(far, 0, -1):
        sums = merge(gathered(*done[s][:2], crossed[s]), groups[s], adds, added)
        if s > 1:
            held, unused = lax.optimization_barrier((done[s - 2][2], sums[0]))
            crossed[s - 2] = over_chip(held)
        adds, added = [left(sums[0])], (0,)
        if len(sums) > 1:
            adds, added = adds + [right(sums[1])], (0, 1)
    [combined] = merge(gathered(*done[0][:2], crossed[0]), groups[0], adds, (0, 0))
    return combined


def solution(mesh):
    placed = (
        P(("dp", "row", "col"), None),
        P(("dp", "row", "col"), None),
        P(("dp", "row", "col"), None),
        P(("row", "col"), None, None),
        P(("row", "col"), None, None),
        P(("row", "col"), None, None),
    )
    return jax.shard_map(
        body, mesh=mesh, in_specs=placed, out_specs=P(("dp", "row", "col"), None), check_vma=False
    )
```

```python
import functools

import jax
import jax.numpy as jnp
from jax import lax
from jax.experimental import pallas as pl
from jax.experimental.pallas import tpu as pltpu
from jax.sharding import PartitionSpec as P

F32 = jnp.float32
BF16 = jnp.bfloat16
LANES = 128
ABSENT = -4096.0
VMEM_BYTES = 24 * 1024 * 1024
ANY = pl.BlockSpec(memory_space=pl.ANY)
LIGHT = pl.CostEstimate(flops=1, transcendentals=0, bytes_accessed=1)


def params(*semantics):
    return pltpu.CompilerParams(dimension_semantics=semantics or None, vmem_limit_bytes=VMEM_BYTES)


def ring(count, step):
    return [(i, (i + step) % count) for i in range(count)]


def swap(count, mask):
    return [(i, i ^ mask) for i in range(count)]


def prep_kernel(tokens_ref, routes_in, gates_in, out_ref, routes_ref, gates_ref, table_ref, sems, *, experts):
    rows, features = tokens_ref.shape
    top = routes_in.shape[0]
    routes_copy = pltpu.make_async_copy(routes_in, routes_ref, sems.at[2])
    gates_copy = pltpu.make_async_copy(gates_in, gates_ref, sems.at[3])
    routes_copy.start()
    gates_copy.start()
    body_copy = pltpu.make_async_copy(tokens_ref, out_ref.at[:, pl.ds(0, features)], sems.at[0])
    body_copy.start()
    routes_copy.wait()
    gates_copy.wait()
    line = lax.broadcasted_iota(jnp.int32, (LANES, rows), 0)
    expert = line % experts
    named = jnp.zeros((LANES, rows), F32)
    gate = jnp.zeros((LANES, rows), F32)
    for k in range(top):
        hit = expert == routes_ref[k : k + 1, :]
        named = jnp.where(hit, 1.0, named)
        gate = jnp.where(hit, gates_ref[k : k + 1, :], gate)
    row_id = lax.broadcasted_iota(jnp.int32, (rows, rows), 0)
    col_id = lax.broadcasted_iota(jnp.int32, (rows, rows), 1)
    earlier = jnp.where(row_id < col_id, 1.0, 0.0).astype(BF16)
    before = jnp.dot(named.astype(BF16), earlier, preferred_element_type=F32)
    slot = jnp.where(named > 0.0, before, ABSENT)
    high = gate.astype(BF16).astype(F32)
    packed = jnp.where(line < experts, slot, jnp.where(line < 2 * experts, high, gate - high))
    table_ref[...] = jnp.transpose(packed).astype(BF16)
    table_copy = pltpu.make_async_copy(table_ref, out_ref.at[:, pl.ds(features, LANES)], sems.at[1])
    table_copy.start()
    body_copy.wait()
    table_copy.wait()


def prep(tokens, routes, gates, experts):
    rows, features = tokens.shape
    far_side = pl.BlockSpec(memory_space=pltpu.HBM)
    top = routes.shape[1]
    return pl.pallas_call(
        functools.partial(prep_kernel, experts=experts),
        out_shape=jax.ShapeDtypeStruct((rows, features + LANES), BF16),
        in_specs=[far_side] * 3,
        out_specs=far_side,
        scratch_shapes=[
            pltpu.VMEM((top, rows), jnp.int32),
            pltpu.VMEM((top, rows), F32),
            pltpu.VMEM((rows, LANES), BF16),
            pltpu.SemaphoreType.DMA((4,)),
        ],
        compiler_params=params(),
        cost_estimate=LIGHT,
        name="prep",
    )(*[pltpu.with_memory_space_constraint(x, pltpu.HBM) for x in (tokens, routes.T, gates.T)])


def column(table, index):
    lane = lax.broadcasted_iota(jnp.int32, table.shape, 1)
    return jnp.sum(jnp.where(lane == index, table, 0.0), axis=1, keepdims=True)


def spread(columns, width, block):
    rows = columns[0].shape[0]
    lane = lax.broadcasted_iota(jnp.int32, (rows, width), 1)
    result = jnp.broadcast_to(columns[-1], (rows, width))
    for k in range(len(columns) - 2, -1, -1):
        result = jnp.where(lane < (k + 1) * block, columns[k], result)
    return result


def near_height(size):
    return size if size % 16 == 0 else 2 * size


def stacked(refs):
    return refs[0][...] if len(refs) == 1 else jnp.concatenate([r[...] for r in refs], axis=0)


def select_kernel(where_ref, *refs, n, mates, cols, capacity):
    data = [refs[:2]] if n == 0 else [(r,) for r in refs[:n]]
    metas = [refs[2:4]] if n == 0 else [(r,) for r in refs[n : 2 * n]]
    n = len(data)
    own_ref, core_ref, cross_ref, hot_ref = refs[-4:]
    width = mates * capacity

    @pl.when(pl.program_id(0) == 0)
    def _():
        for c in range(n):
            table = stacked(metas[c]).astype(F32)
            rows = table.shape[0]
            slots = [column(table, (where_ref[0] ^ k) * cols + where_ref[1]) + k * capacity for k in range(mates)]
            lane = lax.broadcasted_iota(jnp.int32, (rows, width), 1).astype(F32)
            hot_ref[c] = jnp.where(spread(slots, width, capacity) == lane, 1.0, 0.0).astype(BF16)

    picked = [
        lax.dot_general(hot_ref[c], stacked(data[c]), (((0,), (0,)), ((), ())), preferred_element_type=F32)
        for c in range(n)
    ]

    def rows_for(ks):
        parts = [p[k * capacity : (k + 1) * capacity] for k in ks for p in picked]
        return (parts[0] if len(parts) == 1 else jnp.concatenate(parts, axis=0)).astype(BF16)

    own_ref[...] = rows_for((0,))
    core_ref[...] = rows_for((1,))
    cross_ref[...] = rows_for((2, 3))


def select(where, chunks, after, mates, cols, capacity, tokens, tile=1024):
    rows, wide = chunks[0].shape
    pieces = len(chunks)
    halves = pieces == 2 and rows < tokens
    n = 1 if halves else pieces
    features = wide - LANES
    size = n * capacity
    data = pl.BlockSpec((rows, tile), lambda i, w: (0, i))
    meta = pl.BlockSpec((rows, LANES), lambda i, w: (0, features // LANES))
    heights = (size, size, 2 * size)
    return pl.pallas_call(
        functools.partial(select_kernel, n=0 if halves else n, mates=mates, cols=cols, capacity=capacity),
        out_shape=[jax.ShapeDtypeStruct((h, features), BF16) for h in heights],
        grid_spec=pltpu.PrefetchScalarGridSpec(
            num_scalar_prefetch=1,
            grid=(features // tile,),
            in_specs=[data] * pieces + [meta] * pieces + [ANY] * len(after),
            out_specs=[pl.BlockSpec((h, tile), lambda i, w: (0, i)) for h in heights],
            scratch_shapes=[pltpu.VMEM((n, tokens, mates * capacity), BF16)],
        ),
        compiler_params=params("arbitrary"),
        cost_estimate=LIGHT,
        name="select",
    )(where, *chunks, *chunks, *after)


def expert_kernel(own_in, core_in, cross_in, gate_ref, up_ref, down_ref, *refs):
    own_out, core_out, cross_out = refs[-3:]
    size = own_in.shape[0]
    parts = [own_in[...].astype(F32), core_in[...].astype(F32), cross_in[...].astype(F32)[:size]]
    rows = jnp.concatenate(parts, axis=0).astype(BF16)
    gate_part = jnp.dot(rows, gate_ref[0], preferred_element_type=F32)
    up_part = jnp.dot(rows, up_ref[0], preferred_element_type=F32)
    hidden = (gate_part / (1.0 + jnp.exp(-gate_part)) * up_part).astype(BF16)
    result = jnp.dot(hidden, down_ref[0], preferred_element_type=F32)
    own_out[...] = result[:size].astype(BF16)
    core_out[...] = result[size : 2 * size].astype(BF16)
    crossing = jnp.concatenate([result[3 * size :], result[2 * size : 3 * size]], axis=0)
    cross_out[...] = crossing.astype(BF16)


def expert(arrivals, w_gate, w_up, w_down, after):
    size, features = arrivals[0].shape

    def whole(height):
        return pl.BlockSpec((height, features), lambda i: (0, 0))

    heights = (size, size, 2 * size)
    return pl.pallas_call(
        expert_kernel,
        out_shape=[jax.ShapeDtypeStruct((h, features), BF16) for h in heights],
        grid=(1,),
        in_specs=[whole(size), whole(2 * size), whole(near_height(size))]
        + [pl.BlockSpec(memory_space=pltpu.VMEM)] * 3
        + [ANY] * len(after),
        out_specs=[whole(h) for h in heights],
        compiler_params=params("arbitrary"),
        cost_estimate=LIGHT,
        name="expert",
    )(*arrivals, w_gate, w_up, w_down, *after)


def weigh_kernel(where_ref, *refs, n, cols, capacity, experts, order):
    pieces = 2 if n == 0 else n
    blocks, metas = refs[:4], refs[4 : 4 + pieces]
    metas = [metas] if n == 0 else [(m,) for m in metas]
    n = heads = len(metas)
    outs, weight_ref = refs[-1 - heads : -1], refs[-1]
    block = n * capacity
    width = len(order) * block
    tok = weight_ref.shape[1] // 2

    @pl.when(pl.program_id(0) == 0)
    def _():
        for c in range(n):
            table = stacked(metas[c]).astype(F32)
            lane = lax.broadcasted_iota(jnp.int32, (tok, width), 1).astype(F32)
            slots, highs, lows = [], [], []
            for place, k in enumerate(order):
                index = (where_ref[0] ^ k) * cols + where_ref[1]
                slots.append(column(table, index) + (place * n + c) * capacity)
                highs.append(column(table, index + experts))
                lows.append(column(table, index + 2 * experts))
            hit = spread(slots, width, block) == lane
            weight_ref[c, :tok] = jnp.where(hit, spread(highs, width, block), 0.0).astype(BF16)
            weight_ref[c, tok:] = jnp.where(hit, spread(lows, width, block), 0.0).astype(BF16)

    rows = jnp.concatenate([b[...].astype(F32)[:block] for b in blocks], axis=0).astype(BF16)
    for c in range(heads):
        both = jnp.dot(weight_ref[c], rows, preferred_element_type=F32)
        outs[c][...] = (both[:tok] + both[tok:]).astype(outs[c].dtype)


def weigh(where, blocks, chunks, dtype, after, mates, cols, capacity, tokens, tile=1024):
    height, wide = chunks[0].shape
    rows, pieces = tokens, len(chunks)
    halves = pieces == 2 and height < tokens
    n = 1 if halves else pieces
    features = wide - LANES
    size = n * capacity

    def spec(height):
        return pl.BlockSpec((height, tile), lambda i, w: (0, i))

    meta = pl.BlockSpec((height, LANES), lambda i, w: (0, features // LANES))
    return pl.pallas_call(
        functools.partial(
            weigh_kernel,
            n=0 if halves else n,
            cols=cols,
            capacity=capacity,
            experts=mates * cols,
            order=(0, 1, 3, 2),
        ),
        out_shape=[jax.ShapeDtypeStruct((rows, features), dtype)] * n,
        grid_spec=pltpu.PrefetchScalarGridSpec(
            num_scalar_prefetch=1,
            grid=(features // tile,),
            in_specs=[spec(size)] * (mates - 1)
            + [spec(near_height(size))]
            + [meta] * pieces
            + [ANY] * len(after),
            out_specs=[spec(rows)] * n,
            scratch_shapes=[pltpu.VMEM((n, 2 * rows, mates * size), BF16)],
        ),
        compiler_params=params("arbitrary"),
        cost_estimate=LIGHT,
        name="weigh",
    )(where, *blocks, *chunks, *after)


def add_kernel(*refs, heads, added):
    sums, adds, outs = refs[:heads], refs[heads : heads + len(added)], refs[-heads:]
    for c in range(heads):
        total = sums[c][...]
        for add, head in zip(adds, added):
            if head == c:
                total = total + add[...].astype(F32)
        outs[c][...] = total.astype(BF16)


def add_ring(sums, adds, added, tile=1024):
    heads = len(sums)
    rows, features = sums[0].shape
    spec = pl.BlockSpec((rows, tile), lambda i: (0, i))
    return pl.pallas_call(
        functools.partial(add_kernel, heads=heads, added=added),
        out_shape=[jax.ShapeDtypeStruct((rows, features), BF16)] * heads,
        grid=(features // tile,),
        in_specs=[spec] * (heads + len(adds)),
        out_specs=[spec] * heads,
        compiler_params=params("arbitrary"),
        cost_estimate=LIGHT,
        name="add_ring",
    )(*sums, *adds)


def body(tokens, routes, gate_values, w_gate, w_up, w_down):
    tok_rows = tokens.shape[0]
    top_count = routes.shape[1]
    mates = lax.axis_size("row")
    cols = lax.axis_size("col")
    experts = mates * cols
    capacity = 5 * tok_rows * top_count // (4 * experts)
    far = cols // 2
    half = tok_rows // 2
    where = jnp.stack([lax.axis_index("row"), lax.axis_index("col")]).astype(jnp.int32)

    def right(x):
        return lax.ppermute(x, "col", ring(cols, 1))

    def left(x):
        return lax.ppermute(x, "col", ring(cols, -1))

    def over_chip(cross):
        return lax.ppermute(cross, "row", swap(mates, 2))

    def gathered(own, core, crossed):
        size = core.shape[0]
        passed_on = lax.ppermute(crossed[size:], "row", swap(mates, 1))
        return own, lax.ppermute(core, "row", swap(mates, 1)), passed_on, crossed

    last = []

    def pick(chunks):
        own, core, cross = select(where, chunks, last[-1:], mates, cols, capacity, tok_rows)
        last.append(own)
        return own, core, over_chip(cross)

    def settle(own, core, crossed, gate=None):
        if gate is not None:
            crossed, unused = lax.optimization_barrier((crossed, gate))
        both = jnp.concatenate([core, crossed[core.shape[0] :]], axis=0)
        return own, lax.ppermute(both, "row", swap(mates, 1)), crossed

    def run(arrivals):
        out = expert(arrivals, w_gate, w_up, w_down, last[-1:])
        last.append(out[0])
        return out

    def merge(blocks, chunks, adds, added):
        out = weigh(
            where, blocks, chunks, F32 if adds else BF16, last[-1:], mates, cols, capacity, tok_rows
        )
        if adds:
            out = add_ring(out, adds, added)
        last.append(out[0])
        return out

    payload = prep(tokens, routes, gate_values, experts)
    groups, arrived, done = [[payload]], {}, {}
    to_right, to_left = right(payload), left(payload)
    arrived[0] = pick(groups[0])
    for s in range(1, far):
        gate = arrived[0][2] if s == 1 else last[-1]
        from_left, from_right, unused = lax.optimization_barrier((to_right, to_left, gate))
        groups.append([from_left, from_right])
        if s < far - 1:
            to_right, to_left = right(from_left), left(from_right)
        else:
            to_right, to_left = right(from_left[:half]), left(from_right[half:])
        arrived[s] = pick(groups[s])
        if s == far - 1:
            arrived[s - 1] = settle(*arrived[s - 1], last[-1])
        if s == far - 1:
            for early in range(far - 2):
                done[early] = run(settle(*arrived[early]))
    groups.append([to_right, to_left])
    arrived[far] = pick(groups[far])
    done[far - 2] = run(arrived[far - 2])
    for s in (far, far - 1):
        own, core, crossed = arrived[s]
        crossed, unused = lax.optimization_barrier((crossed, done[far - 2][0]))
        done[s] = run(settle(own, core, crossed))

    crossed = {far: over_chip(done[far][2])}
    crossed[far - 1] = over_chip(done[far - 1][2])
    adds, added = [], ()
    for s in range(far, 0, -1):
        sums = merge(gathered(*done[s][:2], crossed[s]), groups[s], adds, added)
        if s > 1:
            held, unused = lax.optimization_barrier((done[s - 2][2], sums[0]))
            crossed[s - 2] = over_chip(held)
        adds, added = [left(sums[0])], (0,)
        if len(sums) > 1:
            adds, added = adds + [right(sums[1])], (0, 1)
    [combined] = merge(gathered(*done[0][:2], crossed[0]), groups[0], adds, (0, 0))
    return combined


def solution(mesh):
    placed = (
        P(("dp", "row", "col"), None),
        P(("dp", "row", "col"), None),
        P(("dp", "row", "col"), None),
        P(("row", "col"), None, None),
        P(("row", "col"), None, None),
        P(("row", "col"), None, None),
    )
    return jax.shard_map(
        body, mesh=mesh, in_specs=placed, out_specs=P(("dp", "row", "col"), None), check_vma=False
    )
```

```python
import functools

import jax
import jax.numpy as jnp
from jax import lax
from jax.experimental import pallas as pl
from jax.experimental.pallas import tpu as pltpu
from jax.sharding import PartitionSpec as P

F32 = jnp.float32
BF16 = jnp.bfloat16
LANES = 128
ABSENT = -4096.0
VMEM_BYTES = 24 * 1024 * 1024
ANY = pl.BlockSpec(memory_space=pl.ANY)
LIGHT = pl.CostEstimate(flops=1, transcendentals=0, bytes_accessed=1)


def params(*semantics):
    return pltpu.CompilerParams(dimension_semantics=semantics or None, vmem_limit_bytes=VMEM_BYTES)


def ring(count, step):
    return [(i, (i + step) % count) for i in range(count)]


def swap(count, mask):
    return [(i, i ^ mask) for i in range(count)]


def prep_kernel(tokens_ref, routes_in, gates_in, out_ref, routes_ref, gates_ref, table_ref, sems, *, experts):
    rows, features = tokens_ref.shape
    top = routes_in.shape[0]
    routes_copy = pltpu.make_async_copy(routes_in, routes_ref, sems.at[2])
    gates_copy = pltpu.make_async_copy(gates_in, gates_ref, sems.at[3])
    routes_copy.start()
    gates_copy.start()
    body_copy = pltpu.make_async_copy(tokens_ref, out_ref.at[:, pl.ds(0, features)], sems.at[0])
    body_copy.start()
    routes_copy.wait()
    gates_copy.wait()
    line = lax.broadcasted_iota(jnp.int32, (LANES, rows), 0)
    expert = line % experts
    named = jnp.zeros((LANES, rows), F32)
    gate = jnp.zeros((LANES, rows), F32)
    for k in range(top):
        hit = expert == routes_ref[k : k + 1, :]
        named = jnp.where(hit, 1.0, named)
        gate = jnp.where(hit, gates_ref[k : k + 1, :], gate)
    row_id = lax.broadcasted_iota(jnp.int32, (rows, rows), 0)
    col_id = lax.broadcasted_iota(jnp.int32, (rows, rows), 1)
    earlier = jnp.where(row_id < col_id, 1.0, 0.0).astype(BF16)
    before = jnp.dot(named.astype(BF16), earlier, preferred_element_type=F32)
    slot = jnp.where(named > 0.0, before, ABSENT)
    high = gate.astype(BF16).astype(F32)
    packed = jnp.where(line < experts, slot, jnp.where(line < 2 * experts, high, gate - high))
    table_ref[...] = jnp.transpose(packed).astype(BF16)
    table_copy = pltpu.make_async_copy(table_ref, out_ref.at[:, pl.ds(features, LANES)], sems.at[1])
    table_copy.start()
    body_copy.wait()
    table_copy.wait()


def prep(tokens, routes, gates, experts):
    rows, features = tokens.shape
    far_side = pl.BlockSpec(memory_space=pltpu.HBM)
    top = routes.shape[1]
    return pl.pallas_call(
        functools.partial(prep_kernel, experts=experts),
        out_shape=jax.ShapeDtypeStruct((rows, features + LANES), BF16),
        in_specs=[far_side] * 3,
        out_specs=far_side,
        scratch_shapes=[
            pltpu.VMEM((top, rows), jnp.int32),
            pltpu.VMEM((top, rows), F32),
            pltpu.VMEM((rows, LANES), BF16),
            pltpu.SemaphoreType.DMA((4,)),
        ],
        compiler_params=params(),
        cost_estimate=LIGHT,
        name="prep",
    )(*[pltpu.with_memory_space_constraint(x, pltpu.HBM) for x in (tokens, routes.T, gates.T)])


def column(table, index):
    lane = lax.broadcasted_iota(jnp.int32, table.shape, 1)
    return jnp.sum(jnp.where(lane == index, table, 0.0), axis=1, keepdims=True)


def spread(columns, width, block):
    rows = columns[0].shape[0]
    lane = lax.broadcasted_iota(jnp.int32, (rows, width), 1)
    result = jnp.broadcast_to(columns[-1], (rows, width))
    for k in range(len(columns) - 2, -1, -1):
        result = jnp.where(lane < (k + 1) * block, columns[k], result)
    return result


def near_height(size):
    return size if size % 16 == 0 else 2 * size


def stacked(refs):
    return refs[0][...] if len(refs) == 1 else jnp.concatenate([r[...] for r in refs], axis=0)


def select_kernel(where_ref, *refs, n, mates, cols, capacity):
    data = [refs[:2]] if n == 0 else [(r,) for r in refs[:n]]
    metas = [refs[2:4]] if n == 0 else [(r,) for r in refs[n : 2 * n]]
    n = len(data)
    own_ref, core_ref, cross_ref, hot_ref = refs[-4:]
    width = mates * capacity

    @pl.when(pl.program_id(0) == 0)
    def _():
        for c in range(n):
            table = stacked(metas[c]).astype(F32)
            rows = table.shape[0]
            slots = [column(table, (where_ref[0] ^ k) * cols + where_ref[1]) + k * capacity for k in range(mates)]
            lane = lax.broadcasted_iota(jnp.int32, (rows, width), 1).astype(F32)
            hot_ref[c] = jnp.where(spread(slots, width, capacity) == lane, 1.0, 0.0).astype(BF16)

    picked = [
        lax.dot_general(hot_ref[c], stacked(data[c]), (((0,), (0,)), ((), ())), preferred_element_type=F32)
        for c in range(n)
    ]

    def rows_for(ks):
        parts = [p[k * capacity : (k + 1) * capacity] for k in ks for p in picked]
        return (parts[0] if len(parts) == 1 else jnp.concatenate(parts, axis=0)).astype(BF16)

    own_ref[...] = rows_for((0,))
    core_ref[...] = rows_for((1,))
    cross_ref[...] = rows_for((2, 3))


def select(where, chunks, after, mates, cols, capacity, tokens, tile=2048):
    rows, wide = chunks[0].shape
    pieces = len(chunks)
    halves = pieces == 2 and rows < tokens
    n = 1 if halves else pieces
    features = wide - LANES
    size = n * capacity
    data = pl.BlockSpec((rows, tile), lambda i, w: (0, i))
    meta = pl.BlockSpec((rows, LANES), lambda i, w: (0, features // LANES))
    heights = (size, size, 2 * size)
    return pl.pallas_call(
        functools.partial(select_kernel, n=0 if halves else n, mates=mates, cols=cols, capacity=capacity),
        out_shape=[jax.ShapeDtypeStruct((h, features), BF16) for h in heights],
        grid_spec=pltpu.PrefetchScalarGridSpec(
            num_scalar_prefetch=1,
            grid=(features // tile,),
            in_specs=[data] * pieces + [meta] * pieces + [ANY] * len(after),
            out_specs=[pl.BlockSpec((h, tile), lambda i, w: (0, i)) for h in heights],
            scratch_shapes=[pltpu.VMEM((n, tokens, mates * capacity), BF16)],
        ),
        compiler_params=params("arbitrary"),
        cost_estimate=LIGHT,
        name="select",
    )(where, *chunks, *chunks, *after)


def expert_kernel(own_in, core_in, cross_in, gate_ref, up_ref, down_ref, *refs):
    own_out, core_out, cross_out = refs[-3:]
    size = own_in.shape[0]
    parts = [own_in[...].astype(F32), core_in[...].astype(F32), cross_in[...].astype(F32)[:size]]
    rows = jnp.concatenate(parts, axis=0).astype(BF16)
    gate_part = jnp.dot(rows, gate_ref[0], preferred_element_type=F32)
    up_part = jnp.dot(rows, up_ref[0], preferred_element_type=F32)
    hidden = (gate_part / (1.0 + jnp.exp(-gate_part)) * up_part).astype(BF16)
    result = jnp.dot(hidden, down_ref[0], preferred_element_type=F32)
    own_out[...] = result[:size].astype(BF16)
    core_out[...] = result[size : 2 * size].astype(BF16)
    crossing = jnp.concatenate([result[3 * size :], result[2 * size : 3 * size]], axis=0)
    cross_out[...] = crossing.astype(BF16)


def expert(arrivals, w_gate, w_up, w_down, after):
    size, features = arrivals[0].shape

    def whole(height):
        return pl.BlockSpec((height, features), lambda i: (0, 0))

    heights = (size, size, 2 * size)
    return pl.pallas_call(
        expert_kernel,
        out_shape=[jax.ShapeDtypeStruct((h, features), BF16) for h in heights],
        grid=(1,),
        in_specs=[whole(size), whole(2 * size), whole(near_height(size))]
        + [pl.BlockSpec(memory_space=pltpu.VMEM)] * 3
        + [ANY] * len(after),
        out_specs=[whole(h) for h in heights],
        compiler_params=params("arbitrary"),
        cost_estimate=LIGHT,
        name="expert",
    )(*arrivals, w_gate, w_up, w_down, *after)


def weigh_kernel(where_ref, *refs, n, cols, capacity, experts, order):
    pieces = 2 if n == 0 else n
    blocks, metas = refs[:4], refs[4 : 4 + pieces]
    metas = [metas] if n == 0 else [(m,) for m in metas]
    n = heads = len(metas)
    outs, weight_ref = refs[-1 - heads : -1], refs[-1]
    block = n * capacity
    width = len(order) * block
    tok = weight_ref.shape[1] // 2

    @pl.when(pl.program_id(0) == 0)
    def _():
        for c in range(n):
            table = stacked(metas[c]).astype(F32)
            lane = lax.broadcasted_iota(jnp.int32, (tok, width), 1).astype(F32)
            slots, highs, lows = [], [], []
            for place, k in enumerate(order):
                index = (where_ref[0] ^ k) * cols + where_ref[1]
                slots.append(column(table, index) + (place * n + c) * capacity)
                highs.append(column(table, index + experts))
                lows.append(column(table, index + 2 * experts))
            hit = spread(slots, width, block) == lane
            weight_ref[c, :tok] = jnp.where(hit, spread(highs, width, block), 0.0).astype(BF16)
            weight_ref[c, tok:] = jnp.where(hit, spread(lows, width, block), 0.0).astype(BF16)

    rows = jnp.concatenate([b[...].astype(F32)[:block] for b in blocks], axis=0).astype(BF16)
    for c in range(heads):
        both = jnp.dot(weight_ref[c], rows, preferred_element_type=F32)
        outs[c][...] = (both[:tok] + both[tok:]).astype(outs[c].dtype)


def weigh(where, blocks, chunks, dtype, after, mates, cols, capacity, tokens, tile=2048):
    height, wide = chunks[0].shape
    rows, pieces = tokens, len(chunks)
    halves = pieces == 2 and height < tokens
    n = 1 if halves else pieces
    features = wide - LANES
    size = n * capacity

    def spec(height):
        return pl.BlockSpec((height, tile), lambda i, w: (0, i))

    meta = pl.BlockSpec((height, LANES), lambda i, w: (0, features // LANES))
    return pl.pallas_call(
        functools.partial(
            weigh_kernel,
            n=0 if halves else n,
            cols=cols,
            capacity=capacity,
            experts=mates * cols,
            order=(0, 1, 3, 2),
        ),
        out_shape=[jax.ShapeDtypeStruct((rows, features), dtype)] * n,
        grid_spec=pltpu.PrefetchScalarGridSpec(
            num_scalar_prefetch=1,
            grid=(features // tile,),
            in_specs=[spec(size)] * (mates - 1)
            + [spec(near_height(size))]
            + [meta] * pieces
            + [ANY] * len(after),
            out_specs=[spec(rows)] * n,
            scratch_shapes=[pltpu.VMEM((n, 2 * rows, mates * size), BF16)],
        ),
        compiler_params=params("arbitrary"),
        cost_estimate=LIGHT,
        name="weigh",
    )(where, *blocks, *chunks, *after)


def add_kernel(*refs, heads, added):
    sums, adds, outs = refs[:heads], refs[heads : heads + len(added)], refs[-heads:]
    for c in range(heads):
        total = sums[c][...]
        for add, head in zip(adds, added):
            if head == c:
                total = total + add[...].astype(F32)
        outs[c][...] = total.astype(BF16)


def add_ring(sums, adds, added, tile=2048):
    heads = len(sums)
    rows, features = sums[0].shape
    spec = pl.BlockSpec((rows, tile), lambda i: (0, i))
    return pl.pallas_call(
        functools.partial(add_kernel, heads=heads, added=added),
        out_shape=[jax.ShapeDtypeStruct((rows, features), BF16)] * heads,
        grid=(features // tile,),
        in_specs=[spec] * (heads + len(adds)),
        out_specs=[spec] * heads,
        compiler_params=params("arbitrary"),
        cost_estimate=LIGHT,
        name="add_ring",
    )(*sums, *adds)


def body(tokens, routes, gate_values, w_gate, w_up, w_down):
    tok_rows = tokens.shape[0]
    top_count = routes.shape[1]
    mates = lax.axis_size("row")
    cols = lax.axis_size("col")
    experts = mates * cols
    capacity = 5 * tok_rows * top_count // (4 * experts)
    far = cols // 2
    half = tok_rows // 2
    where = jnp.stack([lax.axis_index("row"), lax.axis_index("col")]).astype(jnp.int32)

    def right(x):
        return lax.ppermute(x, "col", ring(cols, 1))

    def left(x):
        return lax.ppermute(x, "col", ring(cols, -1))

    def over_chip(cross):
        return lax.ppermute(cross, "row", swap(mates, 2))

    def gathered(own, core, crossed):
        size = core.shape[0]
        passed_on = lax.ppermute(crossed[size:], "row", swap(mates, 1))
        return own, lax.ppermute(core, "row", swap(mates, 1)), passed_on, crossed

    last = []

    def pick(chunks):
        own, core, cross = select(where, chunks, last[-1:], mates, cols, capacity, tok_rows)
        last.append(own)
        return own, core, over_chip(cross)

    def settle(own, core, crossed, gate=None):
        if gate is not None:
            crossed, unused = lax.optimization_barrier((crossed, gate))
        both = jnp.concatenate([core, crossed[core.shape[0] :]], axis=0)
        return own, lax.ppermute(both, "row", swap(mates, 1)), crossed

    def run(arrivals):
        out = expert(arrivals, w_gate, w_up, w_down, last[-1:])
        last.append(out[0])
        return out

    def merge(blocks, chunks, adds, added):
        out = weigh(
            where, blocks, chunks, F32 if adds else BF16, last[-1:], mates, cols, capacity, tok_rows
        )
        if adds:
            out = add_ring(out, adds, added)
        last.append(out[0])
        return out

    payload = prep(tokens, routes, gate_values, experts)
    groups, arrived, done = [[payload]], {}, {}
    to_right, to_left = right(payload), left(payload)
    arrived[0] = pick(groups[0])
    for s in range(1, far):
        gate = arrived[0][2] if s == 1 else last[-1]
        from_left, from_right, unused = lax.optimization_barrier((to_right, to_left, gate))
        groups.append([from_left, from_right])
        if s < far - 1:
            to_right, to_left = right(from_left), left(from_right)
        else:
            to_right, to_left = right(from_left[:half]), left(from_right[half:])
        arrived[s] = pick(groups[s])
        if s == far - 1:
            arrived[s - 1] = settle(*arrived[s - 1], last[-1])
        if s == far - 1:
            for early in range(far - 2):
                done[early] = run(settle(*arrived[early]))
    groups.append([to_right, to_left])
    arrived[far] = pick(groups[far])
    done[far - 2] = run(arrived[far - 2])
    for s in (far, far - 1):
        own, core, crossed = arrived[s]
        crossed, unused = lax.optimization_barrier((crossed, done[far - 2][0]))
        done[s] = run(settle(own, core, crossed))

    crossed = {far: over_chip(done[far][2])}
    crossed[far - 1] = over_chip(done[far - 1][2])
    adds, added = [], ()
    for s in range(far, 0, -1):
        sums = merge(gathered(*done[s][:2], crossed[s]), groups[s], adds, added)
        if s > 1:
            held, unused = lax.optimization_barrier((done[s - 2][2], sums[0]))
            crossed[s - 2] = over_chip(held)
        adds, added = [left(sums[0])], (0,)
        if len(sums) > 1:
            adds, added = adds + [right(sums[1])], (0, 1)
    [combined] = merge(gathered(*done[0][:2], crossed[0]), groups[0], adds, (0, 0))
    return combined


def solution(mesh):
    placed = (
        P(("dp", "row", "col"), None),
        P(("dp", "row", "col"), None),
        P(("dp", "row", "col"), None),
        P(("row", "col"), None, None),
        P(("row", "col"), None, None),
        P(("row", "col"), None, None),
    )
    return jax.shard_map(
        body, mesh=mesh, in_specs=placed, out_specs=P(("dp", "row", "col"), None), check_vma=False
    )
```
